32 devices in a mesh: row: 16 (over z, y, x), col: 2 (over core).
Axes of the slice: x: 2, y: 2, z: 4, core: 2. Of those that a mesh axis runs over, the one named last changes fastest.
Arguments:
- samples: bfloat16 [32768, 8192], P('row', 'col'), may hold values from -0.046875 to 0.046875
- targets: float32 [32768, 128], P('row'), may hold values from -6 to 6
- factor_inv: float32 [2, 4096, 4096], P('col', None, 'row'), may hold values from -1 to 1, as said below
Outputs:
- solution: float32 [8192, 128], P('col')
- residual: float32 [32768, 128], P('row')
The draws below stay inside these ranges and needn't reach their ends.
Inputs may be any that keep to these rules, and one draw needn't show every extreme that they name: Each factor_inv[j] is lower triangular with a positive diagonal.
All inputs are finite; a program needn't handle non-finite values.
Results may differ from the reference program's by a relative error of at most 0.0039.
Values sent between devices are 32-bit elements; how exact they have to be, the bound alone decides.
A program may use at most 128 MiB of HBM per device.

```python
import jax
import jax.numpy as jnp
from jax import lax

B = 4096
K = 128
ROUNDS = 3
NBLK = 2
FEAT = 8192
SAMPLES = 32768


def draw_factor_inv(key, part):
    key_low = jax.random.fold_in(key, 11)
    key_diag = jax.random.fold_in(key, 23)
    lower = jax.random.normal(key_low, (NBLK, B, B), jnp.float32) * (0.3 / jnp.sqrt(jnp.float32(B)))
    diag = jax.random.uniform(key_diag, (NBLK, B), jnp.float32, 0.5, 1.0)
    row_ids = lax.broadcasted_iota(jnp.int32, (B, B), 0)
    col_ids = lax.broadcasted_iota(jnp.int32, (B, B), 1)
    below = (row_ids > col_ids)[None, :, :]
    on_diag = (row_ids == col_ids)[None, :, :]
    return jnp.where(below, lower, 0.0) + jnp.where(on_diag, diag[:, :, None], 0.0)


def with_spikes(array, own_key, source, target, blocks, factor):
    def block_of(dim):
        return (jnp.arange(array.shape[dim]) // (array.shape[dim] // blocks)).reshape((-1,) + (1,) * (array.ndim - 1 - dim))

    one_side = jax.random.permutation(own_key, blocks)[block_of(target)]
    far = (block_of(target) + blocks // 2) % blocks
    return jnp.where((block_of(source) == one_side) | (block_of(source) == far), factor * array, array)


def block_levels(key, dims, split, smallest, top_value):
    gain = 1.0
    for position, blocks in split:
        draws = jax.random.uniform(jax.random.fold_in(jax.random.fold_in(key, 6), position), (blocks,), jnp.float32, smallest / len(split), top_value / len(split))
        gain = gain * jnp.repeat(jnp.exp(draws), dims[position] // blocks).reshape((-1,) + (1,) * (len(dims) - 1 - position))
    return gain


def centred(rng, extent, scale, reach, shards=(), dtype=jnp.bfloat16):
    values = jax.random.normal(rng, extent, jnp.float32) * scale
    if len(shards) > 0:
        values = block_levels(rng, extent, shards, -0.22, 0.18) * values
    return jnp.clip(values, min=-reach, max=reach).astype(dtype)


def heavy_noise(key, extent, spread, bound, cuts, heavy, held_as=jnp.bfloat16):
    array = spread * jax.random.normal(key, extent, jnp.float32)
    if cuts:
        array = array * block_levels(key, extent, cuts, -0.22, 0.18)
    return jnp.clip(with_spikes(array, jax.random.fold_in(key, 3), *heavy), -bound, bound).astype(held_as)


def setup_inputs(seed: int = 0) -> dict:
    arg_keys = jax.random.split(jax.random.key(seed), 4)
    samples = heavy_noise(arg_keys[0], (SAMPLES, FEAT), SAMPLES ** -0.5, 0.046875, ((0, 16), (1, 2)), (0, 1, 16, 2.0))
    targets = centred(arg_keys[1], (SAMPLES, K), 1.0, 6.0, ((0, 16),), jnp.float32)
    factor_inv = draw_factor_inv(jax.random.fold_in(arg_keys[3], 71), 0)
    return {"samples": samples, "targets": targets, "factor_inv": factor_inv}


ridge_weight = 0.5


def reference(samples, targets, factor_inv):
    residual = targets
    solution = [jnp.zeros((B, K), jnp.float32) for block in range(NBLK)]
    relaxation = 1.0 / NBLK
    for sweep in range(ROUNDS):
        res16 = residual.astype(jnp.bfloat16)
        total = jnp.zeros(residual.shape, jnp.float32)
        for block in range(NBLK):
            columns = samples[:, block * B:(block + 1) * B]
            grad = jnp.dot(columns.T, res16, preferred_element_type=jnp.float32) - ridge_weight * solution[block]
            image = jnp.dot(factor_inv[block], grad, precision=lax.Precision.HIGHEST)
            update = jnp.dot(factor_inv[block].T, image, precision=lax.Precision.HIGHEST)
            solution[block] = solution[block] + relaxation * update
            total = total + jnp.dot(columns, update.astype(jnp.bfloat16), preferred_element_type=jnp.float32)
        residual = residual - relaxation * total
    return jnp.concatenate(solution, axis=0), residual
```

```python
import jax
import jax.numpy as jnp
from jax import lax
from jax.sharding import PartitionSpec as P

ROUNDS = 3


ridge_weight = 0.5


def run_group(samples, residual, inverse, own_rows, offset, relaxation):
    solution = jnp.zeros((samples.shape[1], residual.shape[1]), jnp.float32)
    for sweep in range(ROUNDS):
        res16 = residual.astype(jnp.bfloat16)
        part_grad = jnp.einsum("rb,rk->bk", samples, res16, preferred_element_type=jnp.float32)
        own_solution = lax.dynamic_slice_in_dim(solution, offset, own_rows, 0)
        grad_own = (
            lax.psum_scatter(part_grad, "row", scatter_dimension=0, tiled=True)
            - ridge_weight * own_solution
        )
        term = jnp.dot(inverse, grad_own, precision=lax.Precision.HIGHEST)
        image = lax.psum(term, "row")
        update_own = jnp.einsum("bc,bk->ck", inverse, image, precision=lax.Precision.HIGHEST)
        update = lax.all_gather(update_own, "row", axis=0, tiled=True)
        solution = solution + relaxation * update
        change = jnp.dot(samples, update.astype(jnp.bfloat16), preferred_element_type=jnp.float32)
        residual = residual - relaxation * lax.psum(change, "col")
    return (solution, residual)


def per_device(samples, targets, factor_inv):
    inverse = factor_inv[0]
    own_rows = inverse.shape[1]
    offset = lax.axis_index("row") * own_rows
    relaxation = 1.0 / lax.axis_size("col")
    solution, residual = run_group(samples, targets, inverse, own_rows, offset, relaxation)
    return (solution, residual)


def solution(mesh):
    in_specs = (P("row", "col"), P("row", None), P("col", None, "row"))
    out_specs = (P("col", None), P("row", None))
    return jax.shard_map(
        per_device, mesh=mesh, in_specs=in_specs, out_specs=out_specs, check_vma=False
    )
```

```python
import functools

import jax
import jax.numpy as jnp
from jax import lax
from jax.experimental import pallas as pl
from jax.experimental.pallas import tpu as pltpu
from jax.sharding import PartitionSpec as P

ROUNDS = 3
PARTS = 4


ridge_weight = 0.5


def bit_orders(nbits):
    if nbits == 4:
        return [(3, 2, 1, 0), (2, 3, 0, 1), (1, 3, 2, 0), (0, 2, 3, 1)]
    return [tuple((nbits - 1 - p - t) % nbits for t in range(nbits)) for p in range(PARTS)]


def exchange_kernel(axis, nbits, reduce, gather, x_ref, out_ref, send_sem, recv_sem, *scratch):
    me = lax.axis_index(axis)
    bits = [lax.rem(lax.div(me, 2**b), 2) for b in range(nbits)]
    partner = [me + (1 - 2 * bits[b]) * 2**b for b in range(nbits)]
    orders = bit_orders(nbits)
    rows = (x_ref if not reduce else out_ref if not gather else x_ref).shape[-2] // PARTS
    span = [pl.ds(p * rows, rows) for p in range(PARTS)]

    def index(p, free, flip=None):
        lead = []
        for b in reversed(range(nbits)):
            if b in free:
                lead.append(slice(None))
            else:
                lead.append(1 - bits[b] if b == flip else bits[b])
        return tuple(lead) + (span[p], slice(None))

    def own(p):
        return index(p, ()) if gather else (span[p], slice(None))

    barrier = pltpu.get_barrier_semaphore()
    for b in range(nbits):
        pl.semaphore_signal(
            barrier, inc=1, device_id={axis: partner[b]}, device_id_type=pl.DeviceIdType.MESH
        )
    pl.semaphore_wait(barrier, nbits)

    def start(p, step, source, target, b):
        copy = pltpu.make_async_remote_copy(
            src_ref=source,
            dst_ref=target,
            send_sem=send_sem.at[p, step],
            recv_sem=recv_sem.at[p, step],
            device_id={axis: partner[b]},
            device_id_type=pl.DeviceIdType.MESH,
        )
        copy.start()
        return copy

    live = [None] * PARTS
    step = 0
    if reduce:
        acc, arrived = scratch[0], scratch[1:]

        def landing(p, t):
            return (slice(None),) * (nbits - 1 - t) + (span[p], slice(None))

        def add(p, t):
            live[p].wait()
            keep = index(p, orders[p][: nbits - 1 - t])
            source = x_ref if t == 0 else acc
            value = source[keep] + arrived[t][landing(p, t)]
            if t == nbits - 1:
                out_ref[own(p)] = value
            else:
                acc[keep] = value

        for t in range(nbits):
            for p in range(PARTS):
                if t > 0:
                    add(p, t - 1)
                b = orders[p][nbits - 1 - t]
                source = x_ref if t == 0 else acc
                live[p] = start(
                    p,
                    step,
                    source.at[index(p, orders[p][: nbits - 1 - t], b)],
                    arrived[t].at[landing(p, t)],
                    b,
                )
            step += 1
    for t in range(nbits if gather else 0):
        for p in range(PARTS):
            if t > 0:
                live[p].wait()
            elif reduce:
                add(p, nbits - 1)
            else:
                out_ref[own(p)] = x_ref[span[p], :]
            piece = out_ref.at[index(p, orders[p][:t])]
            live[p] = start(p, step, piece, piece, orders[p][t])
        step += 1
    for p in range(PARTS):
        if gather:
            live[p].wait()
        else:
            add(p, nbits - 1)


def exchange(x, axis, collective_id, reduce, gather):
    n = lax.axis_size(axis)
    nbits = n.bit_length() - 1
    width = x.shape[1]
    block = x.shape[0] // n if reduce else x.shape[0]
    whole = (2,) * nbits + (block, width)
    scratch = []
    if reduce:
        scratch.append(pltpu.VMEM(whole, jnp.float32))
        for t in range(nbits):
            scratch.append(pltpu.VMEM((2,) * (nbits - 1 - t) + (block, width), jnp.float32))
    steps = nbits * (int(reduce) + int(gather))
    out = pl.pallas_call(
        functools.partial(exchange_kernel, axis, nbits, reduce, gather),
        out_shape=jax.ShapeDtypeStruct(whole if gather else (block, width), jnp.float32),
        in_specs=[pl.BlockSpec(memory_space=pltpu.VMEM)],
        out_specs=pl.BlockSpec(memory_space=pltpu.VMEM),
        scratch_shapes=[
            pltpu.SemaphoreType.DMA((PARTS, steps)),
            pltpu.SemaphoreType.DMA((PARTS, steps)),
        ]
        + scratch,
        compiler_params=pltpu.CompilerParams(
            collective_id=collective_id, has_side_effects=True, vmem_limit_bytes=24 << 20
        ),
    )(x.reshape(whole) if reduce else x)
    return out.reshape(-1, width)


def run_group(samples, residual, inverse, own_rows, offset, relaxation):
    solution = jnp.zeros((samples.shape[1], residual.shape[1]), jnp.float32)
    for sweep in range(ROUNDS):
        res16 = residual.astype(jnp.bfloat16)
        part_grad = jnp.einsum("rb,rk->bk", samples, res16, preferred_element_type=jnp.float32)
        own_solution = lax.dynamic_slice_in_dim(solution, offset, own_rows, 0)
        grad_own = exchange(part_grad, "row", 0, True, False) - ridge_weight * own_solution
        term = jnp.dot(inverse, grad_own, precision=lax.Precision.HIGHEST)
        image = exchange(term, "row", 1, True, True)
        update_own = jnp.einsum("bc,bk->ck", inverse, image, precision=lax.Precision.HIGHEST)
        update = exchange(update_own, "row", 2, False, True)
        solution = solution + relaxation * update
        change = jnp.dot(samples, update.astype(jnp.bfloat16), preferred_element_type=jnp.float32)
        residual = residual - relaxation * exchange(change, "col", 3, True, True)
    return (solution, residual)


def per_device(samples, targets, factor_inv):
    inverse = factor_inv[0]
    own_rows = inverse.shape[1]
    offset = lax.axis_index("row") * own_rows
    relaxation = 1.0 / lax.axis_size("col")
    solution, residual = run_group(samples, targets, inverse, own_rows, offset, relaxation)
    return (solution, residual)


def solution(mesh):
    in_specs = (P("row", "col"), P("row", None), P("col", None, "row"))
    out_specs = (P("col", None), P("row", None))
    return jax.shard_map(
        per_device, mesh=mesh, in_specs=in_specs, out_specs=out_specs, check_vma=False
    )
```

```python
import functools

import jax
import jax.numpy as jnp
from jax import lax
from jax.experimental import pallas as pl
from jax.experimental.pallas import tpu as pltpu
from jax.sharding import PartitionSpec as P

ROUNDS = 3
PARTS = 4


ridge_weight = 0.5


def bit_orders(nbits):
    if nbits == 4:
        return [(3, 2, 1, 0), (2, 3, 0, 1), (1, 3, 2, 0), (0, 2, 3, 1)]
    return [tuple((nbits - 1 - p - t) % nbits for t in range(nbits)) for p in range(PARTS)]


def exchange_kernel(axis, nbits, reduce, gather, x_ref, out_ref, send_sem, recv_sem, *scratch):
    me = lax.axis_index(axis)
    bits = [lax.rem(lax.div(me, 2**b), 2) for b in range(nbits)]
    partner = [me + (1 - 2 * bits[b]) * 2**b for b in range(nbits)]
    orders = bit_orders(nbits)
    rows = (x_ref if not reduce else out_ref if not gather else x_ref).shape[-2] // PARTS
    span = [pl.ds(p * rows, rows) for p in range(PARTS)]

    def index(p, free, flip=None):
        lead = []
        for b in reversed(range(nbits)):
            if b in free:
                lead.append(slice(None))
            else:
                lead.append(1 - bits[b] if b == flip else bits[b])
        return tuple(lead) + (span[p], slice(None))

    def own(p):
        return index(p, ()) if gather else (span[p], slice(None))

    barrier = pltpu.get_barrier_semaphore()
    for b in range(nbits):
        pl.semaphore_signal(
            barrier, inc=1, device_id={axis: partner[b]}, device_id_type=pl.DeviceIdType.MESH
        )
    pl.semaphore_wait(barrier, nbits)

    def start(p, step, source, target, b):
        copy = pltpu.make_async_remote_copy(
            src_ref=source,
            dst_ref=target,
            send_sem=send_sem.at[p, step],
            recv_sem=recv_sem.at[p, step],
            device_id={axis: partner[b]},
            device_id_type=pl.DeviceIdType.MESH,
        )
        copy.start()
        return copy

    live = [None] * PARTS
    step = 0
    if reduce:
        acc, arrived = scratch[0], scratch[1:]

        def landing(p, t):
            return (slice(None),) * (nbits - 1 - t) + (span[p], slice(None))

        def add(p, t):
            live[p].wait()
            keep = index(p, orders[p][: nbits - 1 - t])
            source = x_ref if t == 0 else acc
            value = source[keep] + arrived[t][landing(p, t)]
            if t == nbits - 1:
                out_ref[own(p)] = value
            else:
                acc[keep] = value

        for t in range(nbits):
            for p in range(PARTS):
                if t > 0:
                    add(p, t - 1)
                b = orders[p][nbits - 1 - t]
                source = x_ref if t == 0 else acc
                live[p] = start(
                    p,
                    step,
                    source.at[index(p, orders[p][: nbits - 1 - t], b)],
                    arrived[t].at[landing(p, t)],
                    b,
                )
            step += 1
    for t in range(nbits if gather else 0):
        for p in range(PARTS):
            if t > 0:
                live[p].wait()
            elif reduce:
                add(p, nbits - 1)
            else:
                out_ref[own(p)] = x_ref[span[p], :]
            piece = out_ref.at[index(p, orders[p][:t])]
            live[p] = start(p, step, piece, piece, orders[p][t])
        step += 1
    for p in range(PARTS):
        if gather:
            live[p].wait()
        else:
            add(p, nbits - 1)


def exchange(x, axis, collective_id, reduce, gather):
    n = lax.axis_size(axis)
    nbits = n.bit_length() - 1
    width = x.shape[1]
    block = x.shape[0] // n if reduce else x.shape[0]
    whole = (2,) * nbits + (block, width)
    scratch = []
    if reduce:
        scratch.append(pltpu.VMEM(whole, jnp.float32))
        for t in range(nbits):
            scratch.append(pltpu.VMEM((2,) * (nbits - 1 - t) + (block, width), jnp.float32))
    steps = nbits * (int(reduce) + int(gather))
    out = pl.pallas_call(
        functools.partial(exchange_kernel, axis, nbits, reduce, gather),
        out_shape=jax.ShapeDtypeStruct(whole if gather else (block, width), jnp.float32),
        in_specs=[pl.BlockSpec(memory_space=pltpu.VMEM)],
        out_specs=pl.BlockSpec(memory_space=pltpu.VMEM),
        scratch_shapes=[
            pltpu.SemaphoreType.DMA((PARTS, steps)),
            pltpu.SemaphoreType.DMA((PARTS, steps)),
        ]
        + scratch,
        compiler_params=pltpu.CompilerParams(
            collective_id=collective_id, has_side_effects=True, vmem_limit_bytes=24 << 20
        ),
    )(x.reshape(whole) if reduce else x)
    return out.reshape(-1, width)


def run_group(samples, residual, inverse, own_rows, offset, relaxation):
    solution = jnp.zeros((samples.shape[1], residual.shape[1]), jnp.float32)
    for sweep in range(ROUNDS):
        res16 = residual.astype(jnp.bfloat16)
        part_grad = jnp.einsum("rb,rk->bk", samples, res16, preferred_element_type=jnp.float32)
        own_solution = lax.dynamic_slice_in_dim(solution, offset, own_rows, 0)
        grad_own = exchange(part_grad, "row", 0, True, False) - ridge_weight * own_solution
        term = jnp.dot(inverse, grad_own, precision=lax.Precision.HIGH)
        image = exchange(term, "row", 1, True, True)
        update_own = jnp.einsum("bc,bk->ck", inverse, image, precision=lax.Precision.HIGH)
        update = exchange(update_own, "row", 2, False, True)
        solution = solution + relaxation * update
        change = jnp.dot(samples, update.astype(jnp.bfloat16), preferred_element_type=jnp.float32)
        residual = residual - relaxation * exchange(change, "col", 3, True, True)
    return (solution, residual)


def per_device(samples, targets, factor_inv):
    inverse = factor_inv[0]
    own_rows = inverse.shape[1]
    offset = lax.axis_index("row") * own_rows
    relaxation = 1.0 / lax.axis_size("col")
    solution, residual = run_group(samples, targets, inverse, own_rows, offset, relaxation)
    return (solution, residual)


def solution(mesh):
    in_specs = (P("row", "col"), P("row", None), P("col", None, "row"))
    out_specs = (P("col", None), P("row", None))
    return jax.shard_map(
        per_device, mesh=mesh, in_specs=in_specs, out_specs=out_specs, check_vma=False
    )
```

```python
import functools

import jax
import jax.numpy as jnp
from jax import lax
from jax.experimental import pallas as pl
from jax.experimental.pallas import tpu as pltpu
from jax.sharding import PartitionSpec as P

ROUNDS = 3
PARTS = 4


ridge_weight = 0.5


def bit_orders(nbits):
    if nbits == 4:
        return [(3, 2, 1, 0), (2, 3, 0, 1), (1, 3, 2, 0), (0, 2, 3, 1)]
    return [tuple((nbits - 1 - p - t) % nbits for t in range(nbits)) for p in range(PARTS)]


def exchange_kernel(axis, nbits, reduce, gather, x_ref, out_ref, send_sem, recv_sem, *scratch):
    me = lax.axis_index(axis)
    bits = [lax.rem(lax.div(me, 2**b), 2) for b in range(nbits)]
    partner = [me + (1 - 2 * bits[b]) * 2**b for b in range(nbits)]
    orders = bit_orders(nbits)
    rows = (x_ref if not reduce else out_ref if not gather else x_ref).shape[-2] // PARTS
    span = [pl.ds(p * rows, rows) for p in range(PARTS)]

    def index(p, free, flip=None):
        lead = []
        for b in reversed(range(nbits)):
            if b in free:
                lead.append(slice(None))
            else:
                lead.append(1 - bits[b] if b == flip else bits[b])
        return tuple(lead) + (span[p], slice(None))

    def own(p):
        return index(p, ()) if gather else (span[p], slice(None))

    barrier = pltpu.get_barrier_semaphore()
    for b in range(nbits):
        pl.semaphore_signal(
            barrier, inc=1, device_id={axis: partner[b]}, device_id_type=pl.DeviceIdType.MESH
        )
    pl.semaphore_wait(barrier, nbits)

    def start(p, step, source, target, b):
        copy = pltpu.make_async_remote_copy(
            src_ref=source,
            dst_ref=target,
            send_sem=send_sem.at[p, step],
            recv_sem=recv_sem.at[p, step],
            device_id={axis: partner[b]},
            device_id_type=pl.DeviceIdType.MESH,
        )
        copy.start()
        return copy

    live = [None] * PARTS
    step = 0
    if reduce:
        acc, arrived = scratch[0], scratch[1:]

        def landing(p, t):
            return (slice(None),) * (nbits - 1 - t) + (span[p], slice(None))

        def add(p, t):
            live[p].wait()
            keep = index(p, orders[p][: nbits - 1 - t])
            source = x_ref if t == 0 else acc
            value = source[keep] + arrived[t][landing(p, t)]
            if t == nbits - 1:
                out_ref[own(p)] = value
            else:
                acc[keep] = value

        for t in range(nbits):
            for p in range(PARTS):
                if t > 0:
                    add(p, t - 1)
                b = orders[p][nbits - 1 - t]
                source = x_ref if t == 0 else acc
                live[p] = start(
                    p,
                    step,
                    source.at[index(p, orders[p][: nbits - 1 - t], b)],
                    arrived[t].at[landing(p, t)],
                    b,
                )
            step += 1
    for t in range(nbits if gather else 0):
        for p in range(PARTS):
            if t > 0:
                live[p].wait()
            elif reduce:
                add(p, nbits - 1)
            else:
                out_ref[own(p)] = x_ref[span[p], :]
            piece = out_ref.at[index(p, orders[p][:t])]
            live[p] = start(p, step, piece, piece, orders[p][t])
        step += 1
    for p in range(PARTS):
        if gather:
            live[p].wait()
        else:
            add(p, nbits - 1)


def exchange(x, axis, collective_id, reduce, gather):
    n = lax.axis_size(axis)
    nbits = n.bit_length() - 1
    width = x.shape[1]
    block = x.shape[0] // n if reduce else x.shape[0]
    whole = (2,) * nbits + (block, width)
    scratch = []
    if reduce:
        scratch.append(pltpu.VMEM(whole, jnp.float32))
        for t in range(nbits):
            scratch.append(pltpu.VMEM((2,) * (nbits - 1 - t) + (block, width), jnp.float32))
    steps = nbits * (int(reduce) + int(gather))
    out = pl.pallas_call(
        functools.partial(exchange_kernel, axis, nbits, reduce, gather),
        out_shape=jax.ShapeDtypeStruct(whole if gather else (block, width), jnp.float32),
        in_specs=[pl.BlockSpec(memory_space=pltpu.VMEM)],
        out_specs=pl.BlockSpec(memory_space=pltpu.VMEM),
        scratch_shapes=[
            pltpu.SemaphoreType.DMA((PARTS, steps)),
            pltpu.SemaphoreType.DMA((PARTS, steps)),
        ]
        + scratch,
        compiler_params=pltpu.CompilerParams(
            collective_id=collective_id, has_side_effects=True, vmem_limit_bytes=24 << 20
        ),
    )(x.reshape(whole) if reduce else x)
    return out.reshape(-1, width)


def gradient_kernel(res_ref, samples_ref, out_ref):
    out_ref[...] = jnp.dot(
        res_ref[...], samples_ref[...], preferred_element_type=jnp.float32
    ).T


def gradient(samples, res16):
    rows, features = samples.shape
    width = res16.shape[1]
    tile = min(512, features)
    return pl.pallas_call(
        gradient_kernel,
        grid=(features // tile,),
        out_shape=jax.ShapeDtypeStruct((features, width), jnp.float32),
        in_specs=[
            pl.BlockSpec((width, rows), lambda i: (0, 0)),
            pl.BlockSpec((rows, tile), lambda i: (0, i)),
        ],
        out_specs=pl.BlockSpec((tile, width), lambda i: (i, 0)),
        compiler_params=pltpu.CompilerParams(vmem_limit_bytes=24 << 20),
    )(res16.T, samples)


def halves(x):
    high = x.astype(jnp.bfloat16)
    return high, (x - high.astype(jnp.float32)).astype(jnp.bfloat16)


def term_kernel(inverse_ref, grad_ref, out_ref):
    w_high, w_low = halves(inverse_ref[...])
    g_high, g_low = halves(grad_ref[...])
    dot = functools.partial(jnp.dot, preferred_element_type=jnp.float32)
    out_ref[...] = dot(w_high, g_low) + dot(w_low, g_high) + dot(w_high, g_high)


def factor_term(inverse, grad):
    features, own_rows = inverse.shape
    width = grad.shape[1]
    tile = min(512, features)
    return pl.pallas_call(
        term_kernel,
        grid=(features // tile,),
        out_shape=jax.ShapeDtypeStruct((features, width), jnp.float32),
        in_specs=[
            pl.BlockSpec((tile, own_rows), lambda i: (i, 0)),
            pl.BlockSpec((own_rows, width), lambda i: (0, 0)),
        ],
        out_specs=pl.BlockSpec((tile, width), lambda i: (i, 0)),
        compiler_params=pltpu.CompilerParams(vmem_limit_bytes=24 << 20),
    )(inverse, grad)


def run_group(samples, residual, inverse, own_rows, offset, relaxation):
    solution = jnp.zeros((samples.shape[1], residual.shape[1]), jnp.float32)
    for sweep in range(ROUNDS):
        res16 = residual.astype(jnp.bfloat16)
        part_grad = gradient(samples, res16)
        own_solution = lax.dynamic_slice_in_dim(solution, offset, own_rows, 0)
        grad_own = exchange(part_grad, "row", 0, True, False) - ridge_weight * own_solution
        term = factor_term(inverse, grad_own)
        image = exchange(term, "row", 1, True, True)
        update_own = jnp.einsum("bc,bk->ck", inverse, image, precision=lax.Precision.HIGH)
        update = exchange(update_own, "row", 2, False, True)
        solution = solution + relaxation * update
        change = jnp.dot(samples, update.astype(jnp.bfloat16), preferred_element_type=jnp.float32)
        residual = residual - relaxation * exchange(change, "col", 3, True, True)
    return (solution, residual)


def per_device(samples, targets, factor_inv):
    inverse = factor_inv[0]
    own_rows = inverse.shape[1]
    offset = lax.axis_index("row") * own_rows
    relaxation = 1.0 / lax.axis_size("col")
    solution, residual = run_group(samples, targets, inverse, own_rows, offset, relaxation)
    return (solution, residual)


def solution(mesh):
    in_specs = (P("row", "col"), P("row", None), P("col", None, "row"))
    out_specs = (P("col", None), P("row", None))
    return jax.shard_map(
        per_device, mesh=mesh, in_specs=in_specs, out_specs=out_specs, check_vma=False
    )
```
